32 devices in a mesh: group: 4 (over x, core), inner: 8 (over z, y).
Axes of the slice: x: 2, y: 2, z: 4, core: 2. Of those that a mesh axis runs over, the one named last changes fastest.
Arguments:
- tokens: bfloat16 [2, 2048, 2048], P(None, ('group', 'inner')), may hold values from -6 to 6
- route_weight: float32 [2, 2048, 6], P(None, ('group', 'inner')), may hold values from 0.05 to 0.5
- routes: int32 [2, 2048, 6], P(None, ('group', 'inner')), may hold values from 0 to 63, all different within a row; in each aligned block of 64 rows (0 to 63, 64 to 127, ..., all dimensions but the last counted through in order) at most 6 rows name the same one
- replica: int32 [2, 2048, 6], P(None, ('group', 'inner')), may hold values from 0 to 1
- old_place: int32 [128], replicated, may hold values from 0 to 63, as said below
- new_src: int32 [128], replicated, may hold values from 0 to 127, as said below
- w_in: bfloat16 [128, 2816, 2048], P(('group', 'inner')), may hold values from -0.125 to 0.125
- w_out: bfloat16 [128, 1408, 2048], P(('group', 'inner')), may hold values from -0.15625 to 0.15625
- queries: bfloat16 [2, 32, 16, 576], P(None, 'group'), may hold values from -21 to 21
- latent_cache: bfloat16 [2, 384, 256, 576], P(None, ('group', 'inner')), may hold values from -6 to 6
- block_req: int32 [2, 384], P(None, ('group', 'inner')), may hold values from 0 to 7, as said below
- block_len: int32 [2, 384], P(None, ('group', 'inner')), may hold values from 0 to 256
Outputs:
- moe_out: bfloat16 [2, 2048, 2048], P(None, ('group', 'inner'))
- attention: bfloat16 [2, 32, 16, 512], P(None, 'group')
The draws below stay inside these ranges and needn't reach their ends.
Inputs may be any that keep to these rules, and one draw needn't show every extreme that they name: `routes`: within one batch, in each aligned block of 64 tokens (the tokens of one device) no expert is named by more than 6 tokens; a token names 6 different experts. `old_place`: every expert holds exactly two slots. old_place[new_src] names every expert exactly twice. `block_req`: in each batch and group one request has exactly 8192 positions and the others 1024 to 2048; a request's positions fill whole blocks except its last; blocks with block_len 0 are unused.
All inputs are finite; a program needn't handle non-finite values.
Results may differ from the reference program's by a relative error of at most 0.014.
Values may be sent and summed in bfloat16 or wider, within the bound.
A program may use at most 256 MiB of HBM per device.

```python
import math
import jax
import jax.numpy as jnp
import numpy as np
from jax import lax

D = 2048
FF = 1408
EXPERTS = 64
TOPK = 6
H = 16
LAT = 512
KDIM = 576
SLOTS = 128
TOK_DEV = 64
MOST = 6
TOKENS = 2048
REQ_GROUP = 8
REQS = 32
SPAN = 256
MAXLEN = 8192
LMIN = 1024
LMID = 2048
CH_GROUP = 96
N_GROUP = 4


def place_tables(key):
    base_list = jnp.arange(SLOTS, dtype=jnp.int32) % EXPERTS
    old_place = jax.random.permutation(jax.random.fold_in(key, 101), base_list)
    new_expert = jax.random.permutation(jax.random.fold_in(key, 102), base_list)
    choose_copy = jax.random.randint(jax.random.fold_in(key, 103), (SLOTS,), 0, 2)
    slot_hits = (old_place[:, None] == jnp.arange(EXPERTS, dtype=jnp.int32)[None, :]).astype(jnp.int32)
    replica_rank = jnp.sum((jnp.cumsum(slot_hits, axis=0) - slot_hits) * slot_hits, axis=1)
    matches = (old_place[None, :] == new_expert[:, None]) & (replica_rank[None, :] == choose_copy[:, None])
    new_src = jnp.sum(jnp.where(matches, jnp.arange(SLOTS, dtype=jnp.int32)[None, :], 0), axis=1)
    return (old_place.astype(jnp.int32), new_src.astype(jnp.int32))


def draw_old_place(key, part):
    return place_tables(key)[0]


def draw_new_src(key, part):
    return place_tables(key)[1]


def group_layout(key):
    lengths = jax.random.randint(jax.random.fold_in(key, 1), (REQ_GROUP,), LMIN, LMID + 1)
    longest = jax.random.randint(jax.random.fold_in(key, 2), (), 0, REQ_GROUP)
    lengths = jnp.where(jnp.arange(REQ_GROUP) == longest, MAXLEN, lengths)
    blocks_of = (lengths + SPAN - 1) // SPAN
    end_block = jnp.cumsum(blocks_of)
    start_block = end_block - blocks_of
    indices = jnp.arange(CH_GROUP)
    owner_req = jnp.sum((indices[:, None] >= end_block[None, :]).astype(jnp.int32), axis=1)
    is_used = owner_req < REQ_GROUP
    owner_req = jnp.minimum(owner_req, REQ_GROUP - 1)
    own_onehot = owner_req[:, None] == jnp.arange(REQ_GROUP)[None, :]
    own_start = jnp.sum(jnp.where(own_onehot, start_block[None, :], 0), axis=1)
    own_length = jnp.sum(jnp.where(own_onehot, lengths[None, :], 0), axis=1)
    filled = jnp.where(is_used, jnp.clip(own_length - (indices - own_start) * SPAN, 0, SPAN), 0)
    shuffle = jax.random.permutation(jax.random.fold_in(key, 3), CH_GROUP)
    req_table = jnp.zeros((CH_GROUP,), jnp.int32).at[shuffle].set(jnp.where(is_used, owner_req, 0).astype(jnp.int32))
    len_table = jnp.zeros((CH_GROUP,), jnp.int32).at[shuffle].set(filled.astype(jnp.int32))
    first_block = jnp.sum(jnp.where(indices[None, :] == start_block[:, None], shuffle[None, :], 0), axis=1)
    return (req_table, len_table, first_block.astype(jnp.int32))


def cache_layout(key):
    group_keys = jax.random.split(jax.random.fold_in(key, 17), 2 * N_GROUP)
    return jax.vmap(group_layout)(group_keys)


def draw_block_req(key, part):
    return cache_layout(key)[0].reshape(2, N_GROUP * CH_GROUP)


def draw_block_len(key, part):
    return cache_layout(key)[1].reshape(2, N_GROUP * CH_GROUP)


def draw_latent_cache(key, part):
    base_draw = jnp.clip(jax.random.normal(jax.random.fold_in(key, 41), (2, N_GROUP * CH_GROUP, SPAN, KDIM), jnp.float32), -6.0, 6.0)
    return base_draw.astype(jnp.bfloat16)


def draw_queries(key, part):
    base_draw = jnp.clip(0.6 * jax.random.normal(jax.random.fold_in(key, 43), (2, N_GROUP, REQ_GROUP, H, KDIM), jnp.float32), -3.0, 3.0)
    return base_draw.reshape(2, N_GROUP * REQ_GROUP, H, KDIM).astype(jnp.bfloat16)


def set_ends(result, rng, low, high):
    place = [jax.random.randint(jax.random.fold_in(rng, axis), (), 0, length) for axis, length in enumerate(result.shape)]
    widest = result.shape.index(max(result.shape))
    beside = place[:widest] + [(place[widest] + 1) % result.shape[widest]] + place[widest + 1:]
    return result.at[tuple(place)].set(low).at[tuple(beside)].set(high)


def steps_of(rng, extent, cuts, low, top_value):
    loudness, own = 1.0, jax.random.fold_in(rng, 6)
    for axis_at, blocks in cuts:
        heights = jnp.exp(jax.random.uniform(jax.random.fold_in(own, axis_at), (blocks,), jnp.float32, low / len(cuts), top_value / len(cuts)))
        loudness = loudness * jnp.repeat(heights, extent[axis_at] // blocks).reshape([-1 if axis == axis_at else 1 for axis in range(len(extent))])
    return loudness


def routed_block(own_key, own, number, rows, number_of, top, bound, skew):
    order = jax.random.permutation(own_key, number_of)
    packed, common = portions_of(number_of, rows * top, bound, skew, True), portions_of(number_of, rows * top, bound, skew, False)
    places = jnp.arange(number_of)

    def named(sizes, rotation):
        used = int((sizes > 0).sum())
        fixed = max(1, used // 4)
        shifted = fixed + (places - fixed + rotation * (used - fixed)) % max(1, number_of - fixed)
        return jnp.zeros((number_of,), jnp.int32).at[order[jnp.where(places < fixed, places, shifted)]].set(jnp.asarray(sizes, jnp.int32))

    sizes = jnp.where(number % 4 == 0, named(packed, number // 4), named(common, number - number // 4 - 1))
    mixed = jax.random.permutation(jax.random.fold_in(own, 3), number_of)
    donor, receiver = mixed[0:number_of // 2 * 2:2], mixed[1:number_of // 2 * 2:2]
    margin = jnp.minimum(sizes[donor] - 1, bound - sizes[receiver]) // 2
    margin = jnp.where((donor == order[0]) | (receiver == order[0]) | (sizes[receiver] == 0), 0, jnp.maximum(margin, 0))
    shifted = jax.random.randint(jax.random.fold_in(own, 4), (number_of // 2,), 0, 1 << 20) % (margin + 1)
    sizes = sizes.at[donor].add(-shifted).at[receiver].add(shifted)
    labels = jnp.searchsorted(jnp.cumsum(sizes), jnp.arange(rows * top), side="right").astype(jnp.int32)
    table = labels.reshape(top, rows).T
    table = table[jax.random.permutation(jax.random.fold_in(own, 1), rows)]
    rotation = jax.random.randint(jax.random.fold_in(own, 2), (rows, 1), 0, top)
    return jnp.take_along_axis(table, (jnp.arange(top)[None, :] + rotation) % top, axis=1)


def portions_of(count, total, bound, lean, full):
    portions = [(1 << 20) // math.isqrt(grade ** lean) + 1 for grade in range(1, count + 1)]
    largest = bound if full else min(bound, max(-(-total // count), total * portions[0] // sum(portions)))
    least = 1 if total - largest >= count - 1 else 0
    given, spare = [largest] + [least] * (count - 1), total - largest - least * (count - 1)
    while spare > 0:
        free = [i for i in range(1, count) if given[i] < largest] or [i for i in range(1, count) if given[i] < bound]
        mass, left = sum([portions[i] for i in free]), spare
        for i in free:
            more = min(bound - given[i], max(1, left * portions[i] // mass), spare)
            given[i] = given[i] + more
            spare = spare - more
    return np.array(given)


def noise(stream_key, shape, spread, reach, cuts=(), kind=jnp.bfloat16):
    factor_of = steps_of(stream_key, shape, cuts, -0.22, 0.18) if cuts else 1.0
    values = jax.random.normal(stream_key, shape, jnp.float32) * spread * factor_of
    return jnp.minimum(jnp.maximum(values, -reach), reach).astype(kind)


def setup_inputs(seed: int = 0) -> dict:
    key_of = jax.random.split(jax.random.key(seed), 13)
    tokens = noise(key_of[0], (2, TOKENS, D), 1.0, 6.0, ((1, 32),))
    route_weight = jnp.clip(jnp.exp(math.log(0.5) - 2.3025851 * jax.random.uniform(key_of[1], (2, TOKENS, TOPK), jnp.float32) ** steps_of(key_of[1], (2, TOKENS, TOPK), ((1, 32),), -0.2, 0.2)), 0.05, 0.5)
    routes_keys = jax.random.split(jax.random.fold_in(key_of[2], 1), 2 * TOKENS // TOK_DEV)
    routes_turns = jax.random.permutation(jax.random.fold_in(key_of[2], 3), 2 * TOKENS // TOK_DEV)
    routes = jax.vmap(lambda own, number: routed_block(jax.random.fold_in(key_of[2], 2), own, number, TOK_DEV, EXPERTS, TOPK, MOST, 2))(routes_keys, routes_turns).reshape((2, TOKENS, TOPK))
    replica = set_ends(jax.random.randint(key_of[3], (2, TOKENS, TOPK), 0, 2), jax.random.fold_in(key_of[3], 1), 0, 1).astype(jnp.int32)
    old_place = draw_old_place(jax.random.fold_in(key_of[12], 71), 0)
    new_src = draw_new_src(jax.random.fold_in(key_of[12], 71), 0)
    w_in = noise(key_of[6], (SLOTS, 2 * FF, D), D ** -0.5, 0.125, ((0, 32),))
    w_out = noise(key_of[7], (SLOTS, FF, D), FF ** -0.5, 0.15625, ((0, 32),))
    queries = draw_queries(jax.random.fold_in(key_of[12], 71), 0)
    latent_cache = draw_latent_cache(jax.random.fold_in(key_of[12], 71), 0)
    block_req = draw_block_req(jax.random.fold_in(key_of[12], 71), 0)
    block_len = draw_block_len(jax.random.fold_in(key_of[12], 71), 0)
    return dict(tokens=tokens, route_weight=route_weight, routes=routes, replica=replica, old_place=old_place, new_src=new_src, w_in=w_in, w_out=w_out, queries=queries, latent_cache=latent_cache, block_req=block_req, block_len=block_len)


score_scale = 192.0 ** -0.5
floor_value = -1.0e30
block_rows = 64


def block_attention(queries, latent_cache, block_req, block_len, latent):
    requests, head_count, feat_width = queries.shape
    blocks, cache_rows, _ = latent_cache.shape
    belongs = block_req[:, None] == jnp.arange(requests, dtype=jnp.int32)[None, :]
    chosen = jnp.dot(belongs.astype(jnp.bfloat16), queries.reshape(requests, head_count * feat_width), preferred_element_type=jnp.float32)
    chosen = chosen.astype(jnp.bfloat16).reshape(blocks, head_count, feat_width)
    scores = jnp.einsum("chk,cpk->chp", chosen.astype(jnp.float32), latent_cache.astype(jnp.float32)) * score_scale
    live_rows = jnp.arange(cache_rows, dtype=jnp.int32)[None, :] < block_len[:, None]
    scores = jnp.where(live_rows[:, None, :], scores, floor_value)
    block_max = jnp.max(scores, axis=2)
    req_max = jnp.max(jnp.where(belongs[:, :, None], block_max[:, None, :], floor_value), axis=0)
    own_max = jnp.sum(jnp.where(belongs[:, :, None], req_max[None, :, :], 0.0), axis=1)
    exp_scores = jnp.where(live_rows[:, None, :], jnp.exp(scores - own_max[:, :, None]), 0.0)
    block_total = jnp.sum(exp_scores, axis=2)
    weights = exp_scores.astype(jnp.bfloat16)
    block_out = jnp.einsum("chp,cpl->chl", weights.astype(jnp.float32), latent_cache[:, :, :latent].astype(jnp.float32))
    belongs_f = belongs.astype(jnp.float32)
    req_total = jnp.einsum("cr,ch->rh", belongs_f, block_total, precision=lax.Precision.HIGHEST)
    req_out = jnp.einsum("cr,chl->rhl", belongs_f, block_out, precision=lax.Precision.HIGHEST)
    return req_max, req_total, req_out


def slot_of_route(expert_of_slot, routes, replica):
    slot_count = expert_of_slot.shape[0]
    slot_hits = (expert_of_slot[:, None] == jnp.arange(EXPERTS, dtype=jnp.int32)[None, :]).astype(jnp.int32)
    replica_rank = jnp.sum((jnp.cumsum(slot_hits, axis=0) - slot_hits) * slot_hits, axis=1)
    flat_expert = routes.reshape(-1)
    flat_replica = replica.reshape(-1)
    matches = (expert_of_slot[None, :] == flat_expert[:, None]) & (replica_rank[None, :] == flat_replica[:, None])
    return jnp.sum(jnp.where(matches, jnp.arange(slot_count, dtype=jnp.int32)[None, :], 0), axis=1).astype(jnp.int32)


def moe_reference(tokens, route_weight, target, w_in, w_out):
    row_total = target.shape[0]
    feat_width = tokens.shape[1]
    token_rows = jnp.repeat(tokens, TOPK, axis=0)
    sorted_idx = jnp.argsort(target, stable=True).astype(jnp.int32)
    ordered = jnp.concatenate([token_rows[sorted_idx], jnp.zeros((block_rows, feat_width), token_rows.dtype)])
    counts = jnp.sum((target[:, None] == jnp.arange(SLOTS, dtype=jnp.int32)[None, :]).astype(jnp.int32), axis=0).astype(jnp.int32)
    starts = (jnp.cumsum(counts) - counts).astype(jnp.int32)

    def per_slot(results, slot_id):
        start_row = starts[slot_id]
        row_count = counts[slot_id]
        weight_in = w_in[slot_id]
        weight_out = w_out[slot_id]

        def going(loop_state):
            return loop_state[0] * block_rows < row_count

        def step(loop_state):
            turn_index, buffer_rows = loop_state
            begin_row = (start_row + turn_index * block_rows).astype(jnp.int32)
            piece_rows = lax.dynamic_slice_in_dim(ordered, begin_row, block_rows, 0)
            gate_up = jnp.dot(piece_rows, weight_in.T, preferred_element_type=jnp.float32)
            hidden = (jax.nn.silu(gate_up[:, :FF]) * gate_up[:, FF:]).astype(jnp.bfloat16)
            made_rows = jnp.dot(hidden, weight_out, preferred_element_type=jnp.float32).astype(jnp.bfloat16)
            keep_rows = (jnp.arange(block_rows, dtype=jnp.int32) + turn_index * block_rows) < row_count
            current = lax.dynamic_slice_in_dim(buffer_rows, begin_row, block_rows, 0)
            buffer_rows = lax.dynamic_update_slice_in_dim(buffer_rows, jnp.where(keep_rows[:, None], made_rows, current), begin_row, 0)
            return turn_index + 1, buffer_rows

        _, results = lax.while_loop(going, step, (jnp.array(0, jnp.int32), results))
        return results, None

    results = jnp.zeros((row_total + block_rows, feat_width), jnp.bfloat16)
    results, _ = lax.scan(per_slot, results, jnp.arange(SLOTS, dtype=jnp.int32))
    made_all = jnp.zeros((row_total, feat_width), jnp.bfloat16).at[sorted_idx].set(results[:row_total])
    combined = jnp.sum(made_all.astype(jnp.float32).reshape(-1, TOPK, feat_width) * route_weight[:, :, None], axis=1)
    return combined.astype(jnp.bfloat16)


def reference(tokens, route_weight, routes, replica, old_place, new_src, w_in, w_out, queries, latent_cache, block_req, block_len):
    slot_first = slot_of_route(old_place, routes[0], replica[0])
    new_expert = old_place[new_src]
    slot_second = slot_of_route(new_expert, routes[1], replica[1])
    batch_one = moe_reference(tokens[0], route_weight[0], slot_first, w_in, w_out)
    batch_two = moe_reference(tokens[1], route_weight[1], new_src[slot_second].astype(jnp.int32), w_in, w_out)
    moe_out = jnp.stack([batch_one, batch_two])
    group_queries = queries.reshape(2 * N_GROUP, REQ_GROUP, H, KDIM)
    group_cache = latent_cache.reshape(2 * N_GROUP, CH_GROUP, SPAN, KDIM)
    group_req = block_req.reshape(2 * N_GROUP, CH_GROUP)
    group_len = block_len.reshape(2 * N_GROUP, CH_GROUP)

    def one_group(inputs):
        req_max, req_total, req_out = block_attention(inputs[0], inputs[1], inputs[2], inputs[3], LAT)
        return (req_out / req_total[:, :, None]).astype(jnp.bfloat16)

    attention = lax.map(one_group, (group_queries, group_cache, group_req, group_len))
    return moe_out, attention.reshape(2, REQS, H, LAT)
```

```python
from functools import partial

import jax
import jax.numpy as jnp
from jax import lax
from jax.experimental import pallas as pl
from jax.experimental.pallas import tpu as pltpu
from jax.sharding import PartitionSpec as P

MESH = pl.DeviceIdType.MESH
FF = 1408
EXPERTS = 64
TOPK = 6
LAT = 512
MOST = 6
CHUNKS = 4


score_scale = 192.0 ** (-0.5)
floor_value = -1e30


def block_attention(queries, latent_cache, block_req, block_len, latent):
    requests, head_count, feat_width = queries.shape
    blocks, cache_rows, _ = latent_cache.shape
    belongs = block_req[:, None] == jnp.arange(requests, dtype=jnp.int32)[None, :]
    chosen = jnp.dot(
        belongs.astype(jnp.bfloat16),
        queries.reshape(requests, head_count * feat_width),
        preferred_element_type=jnp.float32,
    )
    chosen = chosen.astype(jnp.bfloat16).reshape(blocks, head_count, feat_width)
    scores = (
        jnp.einsum("chk,cpk->chp", chosen, latent_cache, preferred_element_type=jnp.float32)
        * score_scale
    )
    live_rows = jnp.arange(cache_rows, dtype=jnp.int32)[None, :] < block_len[:, None]
    scores = jnp.where(live_rows[:, None, :], scores, floor_value)
    block_max = jnp.max(scores, axis=2)
    req_max = jnp.max(jnp.where(belongs[:, :, None], block_max[:, None, :], floor_value), axis=0)
    own_max = jnp.sum(jnp.where(belongs[:, :, None], req_max[None, :, :], 0.0), axis=1)
    exp_scores = jnp.where(live_rows[:, None, :], jnp.exp(scores - own_max[:, :, None]), 0.0)
    block_total = jnp.sum(exp_scores, axis=2)
    weights = exp_scores.astype(jnp.bfloat16)
    block_out = jnp.einsum(
        "chp,cpl->chl", weights, latent_cache[:, :, :latent], preferred_element_type=jnp.float32
    )
    belongs_f = belongs.astype(jnp.float32)
    req_total = jnp.einsum("cr,ch->rh", belongs_f, block_total, precision=lax.Precision.HIGHEST)
    req_out = jnp.einsum("cr,chl->rhl", belongs_f, block_out, precision=lax.Precision.HIGHEST)
    return (req_max, req_total, req_out)


def join_attention(req_max, req_total, req_out, axis):
    n = lax.axis_size(axis)
    batches, requests, heads, latent = req_out.shape
    share = batches * requests * heads // n
    stats = jnp.stack([req_max.reshape(n, share), req_total.reshape(n, share)], axis=1)
    parts = req_out.astype(jnp.bfloat16).reshape(n, share, latent)
    stats = lax.all_to_all(stats, axis, split_axis=0, concat_axis=0, tiled=True)
    parts = lax.all_to_all(parts, axis, split_axis=0, concat_axis=0, tiled=True)
    joint = jnp.max(stats[:, 0], axis=0)
    scale = jnp.exp(stats[:, 0] - joint[None])
    total = jnp.sum(stats[:, 1] * scale, axis=0)
    summed = jnp.sum(parts.astype(jnp.float32) * scale[..., None], axis=0)
    own = (summed / total[:, None]).astype(jnp.bfloat16)
    whole = lax.all_gather(own, axis, axis=0, tiled=True)
    return whole.reshape(batches, requests, heads, latent)


def replica_keys(expert_of_slot):
    slots = expert_of_slot.shape[0]
    index = jnp.arange(slots, dtype=jnp.int32)
    earlier = (expert_of_slot[None, :] == expert_of_slot[:, None]) & (index[None, :] < index[:, None])
    return expert_of_slot * 2 + jnp.sum(earlier.astype(jnp.int32), axis=1)


def table_lookup(indices, lookup_table):
    matches = indices[:, None] == jnp.arange(lookup_table.shape[0], dtype=jnp.int32)[None, :]
    return jnp.sum(jnp.where(matches, lookup_table[None, :], 0), axis=1)


def places(depth, n_inner):
    width = n_inner // depth
    g, i = lax.axis_index("group"), lax.axis_index("inner")
    z, y = i // width, lax.rem(i, width)
    line = lambda p: (g, p * width + y)
    plane = lambda p: (p // width, z * width + lax.rem(p, width))
    return z, g * width + y, line, plane


def greet(partners):
    barrier = pltpu.get_barrier_semaphore()
    for device in partners:
        pl.semaphore_signal(barrier, inc=1, device_id=device, device_id_type=MESH)
    pl.semaphore_wait(barrier, len(partners))


def remote(src, dst, send, recv, device):
    return pltpu.make_async_remote_copy(
        src_ref=src, dst_ref=dst, send_sem=send, recv_sem=recv, device_id=device, device_id_type=MESH
    )


def dispatch_kernel(depth, n_inner, planes, tok, row, out, gat, tab, box, zs, zr, ps, pr, ls):
    z, me, line, plane = places(depth, n_inner)
    line_to = [lax.rem(z + k, depth) for k in range(1, depth)]
    plane_to = [lax.rem(me + k, planes) for k in range(1, planes)]
    greet([line(p) for p in line_to] + [plane(p) for p in plane_to])
    chunk = gat.shape[3]
    per_box = tab.shape[0] // planes
    flights = []
    for c in range(CHUNKS):
        flight = []
        for k, p in enumerate(line_to):
            copy = remote(
                tok.at[:, pl.ds(c * chunk, chunk)], gat.at[c, z], zs.at[c, k], zr.at[c, k], line(p)
            )
            copy.start()
            flight.append(copy)
        flights.append(flight)
    for c in range(CHUNKS):
        gat[c, z] = tok[:, c * chunk : (c + 1) * chunk]
    step = 256

    def fill(t, carry):
        rows = lax.broadcasted_iota(jnp.int32, (step, tab.shape[1]), 0) + t * step
        total = jnp.zeros((step, tab.shape[1]), jnp.float32)
        for k in range(TOPK):
            total = total + jnp.where(rows == row[k : k + 1, :], 1.0, 0.0)
        tab[pl.ds(pl.multiple_of(t * step, step), step), :] = total.astype(jnp.bfloat16)
        return carry

    lax.fori_loop(0, tab.shape[0] // step, fill, 0)
    sends = []
    for c in range(CHUNKS):
        for copy in flights[c]:
            copy.wait_recv()
        held = gat[c].reshape(tab.shape[1], chunk)

        def build(p, carry):
            table = tab[pl.ds(pl.multiple_of(p * per_box, 16), per_box), :]
            made = jnp.dot(table, held, preferred_element_type=jnp.float32).astype(jnp.bfloat16)
            box[c, p] = made.reshape(box.shape[2:])
            return carry

        lax.fori_loop(0, planes, build, 0)
        for k, p in enumerate(plane_to):
            copy = remote(box.at[c, p], out.at[c, :, me], ps.at[c, k], pr.at[c, k], plane(p))
            copy.start()
            sends.append(copy)
        own = pltpu.make_async_copy(box.at[c, me], out.at[c, :, me], ls.at[c])
        own.start()
        sends.append(own)
    for flight in flights:
        for copy in flight:
            copy.wait_send()
    for copy in sends:
        copy.wait()


def return_kernel(
    depth, n_inner, planes, served, row, weight, out, got, high, low, part, pbuf, own, back, ps, pr, ls, zs, zr
):
    z, me, line, plane = places(depth, n_inner)
    line_to = [lax.rem(z + k, depth) for k in range(1, depth)]
    plane_to = [lax.rem(me + k, planes) for k in range(1, planes)]
    greet([line(p) for p in line_to] + [plane(p) for p in plane_to])
    chunk = got.shape[-1]
    flights = []
    for c in range(CHUNKS):
        flight = []
        for k, p in enumerate(plane_to):
            copy = remote(served.at[c, :, p], got.at[c, me], ps.at[c, k], pr.at[c, k], plane(p))
            copy.start()
            flight.append(copy)
        kept = pltpu.make_async_copy(served.at[c, :, me], got.at[c, me], ls.at[c])
        kept.start()
        flight.append(kept)
        flights.append(flight)
    tokens, rows = high.shape
    step = 256
    for t in range(rows // step):
        cols = lax.broadcasted_iota(jnp.int32, (tokens, step), 1) + t * step
        total = jnp.zeros((tokens, step), jnp.float32)
        for k in range(TOPK):
            total = total + jnp.where(cols == row[:, k : k + 1], weight[:, k : k + 1], 0.0)
        upper = total.astype(jnp.bfloat16)
        high[:, t * step : (t + 1) * step] = upper
        low[:, t * step : (t + 1) * step] = (total - upper.astype(jnp.float32)).astype(jnp.bfloat16)
    sends = []
    for c in range(CHUNKS):
        for copy in flights[c]:
            copy.wait()
        held = got[c].reshape(rows, chunk)
        made = jnp.dot(high[...], held, preferred_element_type=jnp.float32)
        made = made + jnp.dot(low[...], held, preferred_element_type=jnp.float32)
        part[...] = made.reshape(part.shape)
        pbuf[c] = part[...].astype(jnp.bfloat16)
        own[c] = part[z]
        flight = []
        for k, p in enumerate(line_to):
            copy = remote(pbuf.at[c, p], back.at[c, z], zs.at[c, k], zr.at[c, k], line(p))
            copy.start()
            flight.append(copy)
        sends.append(flight)
    for c in range(CHUNKS):
        for copy in sends[c]:
            copy.wait()
        total = own[c]
        for p in line_to:
            total = total + back[c, p].astype(jnp.float32)
        out[:, c * chunk : (c + 1) * chunk] = total.astype(jnp.bfloat16)


def expert_kernel(tile, halves, x, w_gate_up, w_out, out, acc):
    half = pl.program_id(1)
    rows = x.shape[2]
    chunk = x.shape[3]
    for t in range(rows // tile):
        at = slice(t * tile, (t + 1) * tile)
        arrived = jnp.concatenate([x[c, 0, at, :] for c in range(CHUNKS)], axis=1)
        contract = (((1,), (1,)), ((), ()))
        gate = lax.dot_general(arrived, w_gate_up[0, 0], contract, preferred_element_type=jnp.float32)
        up = lax.dot_general(arrived, w_gate_up[0, 1], contract, preferred_element_type=jnp.float32)
        hidden = (gate / (1.0 + jnp.exp(-gate)) * up).astype(jnp.bfloat16)
        made = jnp.dot(hidden, w_out[0], preferred_element_type=jnp.float32)

        @pl.when(half == 0)
        def _():
            acc[at, :] = made

        @pl.when(half == halves - 1)
        def _():
            total = acc[at, :] + made
            for c in range(CHUNKS):
                out[c, 0, at, :] = total[:, c * chunk : (c + 1) * chunk].astype(jnp.bfloat16)


def moe(tokens, route_weight, slots, w_in, w_out):
    n_group, n_inner = lax.axis_size("group"), lax.axis_size("inner")
    batches, tok_count, width = tokens.shape
    slot_dev = w_in.shape[0]
    depth = 4 if n_inner % 4 == 0 else 1
    n_width = n_inner // depth
    planes = n_group * n_width
    box_rows = batches * depth * MOST
    rows = planes * slot_dev * box_rows
    count = depth * batches * tok_count
    chunk = width // CHUNKS
    order = jnp.arange(tok_count * TOPK, dtype=jnp.int32)
    same = (slots[:, :, None] == slots[:, None, :]) & (order[None, None, :] < order[None, :, None])
    position = jnp.sum(same.astype(jnp.int32), axis=2)
    code = (slots * MOST + position).reshape(batches, tok_count, TOPK)
    meta = jnp.stack([code.astype(jnp.float32), route_weight])
    lines = [[p * n_width + y for p in range(depth)] for y in range(n_width)]
    meta = lax.all_gather(meta, "inner", axis_index_groups=lines)
    code = meta[:, 0].astype(jnp.int32)
    target, position = code // MOST, code % MOST
    device, local_slot = target // slot_dev, target % slot_dev
    dev_group, dev_inner = device // n_inner, device % n_inner
    plane = dev_group * n_width + dev_inner % n_width
    source = jnp.arange(depth, dtype=jnp.int32)[:, None, None, None]
    batch = jnp.arange(batches, dtype=jnp.int32)[None, :, None, None]
    row = (plane * slot_dev + local_slot) * box_rows + (source * batches + batch) * MOST + position
    row = jnp.where(dev_inner // n_width == lax.axis_index("inner") // n_width, row, -1)
    row = jnp.pad(row.reshape(count, TOPK), ((0, 0), (0, 2)), constant_values=-1)
    weight = jnp.pad(meta[:, 1].reshape(count, TOPK), ((0, 0), (0, 2)))
    vmem, hbm = pl.BlockSpec(memory_space=pltpu.VMEM), pl.BlockSpec(memory_space=pl.ANY)
    sem = pltpu.SemaphoreType.DMA
    arrived = pl.pallas_call(
        partial(dispatch_kernel, depth, n_inner, planes),
        out_shape=jax.ShapeDtypeStruct((CHUNKS, slot_dev, planes, box_rows, chunk), jnp.bfloat16),
        in_specs=[vmem, vmem],
        out_specs=hbm,
        scratch_shapes=[
            pltpu.VMEM((CHUNKS, depth, batches * tok_count, chunk), jnp.bfloat16),
            pltpu.VMEM((rows, count), jnp.bfloat16),
            pltpu.VMEM((CHUNKS, planes, slot_dev, box_rows, chunk), jnp.bfloat16),
            sem((CHUNKS, depth)),
            sem((CHUNKS, depth)),
            sem((CHUNKS, planes)),
            sem((CHUNKS, planes)),
            sem((CHUNKS,)),
        ],
        compiler_params=pltpu.CompilerParams(
            collective_id=1, has_side_effects=True, vmem_limit_bytes=40 * 2**20
        ),
        name="dispatch",
    )(tokens.reshape(batches * tok_count, width), row.T)
    halves = 2
    slot_rows = planes * box_rows
    tile = 384 if slot_rows % 384 == 0 else slot_rows
    mode = {} if slot_rows <= 384 else {"pipeline_mode": pl.Buffered(1)}
    part_ff = FF // halves
    act = pl.BlockSpec((CHUNKS, 1, slot_rows, chunk), lambda s, h: (0, s, 0, 0), **mode)
    served = pl.pallas_call(
        partial(expert_kernel, tile, halves),
        grid=(slot_dev, halves),
        out_shape=jax.ShapeDtypeStruct((CHUNKS, slot_dev, slot_rows, chunk), jnp.bfloat16),
        in_specs=[
            act,
            pl.BlockSpec((1, 2, part_ff, width), lambda s, h: (s, 0, h, 0)),
            pl.BlockSpec((1, part_ff, width), lambda s, h: (s, h, 0)),
        ],
        out_specs=act,
        scratch_shapes=[pltpu.VMEM((slot_rows, width), jnp.float32)],
        compiler_params=pltpu.CompilerParams(
            vmem_limit_bytes=60 * 2**20, dimension_semantics=("arbitrary", "arbitrary")
        ),
        cost_estimate=pl.CostEstimate(
            flops=6 * slot_dev * slot_rows * FF * width,
            bytes_accessed=6 * slot_dev * FF * width,
            transcendentals=0,
        ),
        name="experts",
    )(
        arrived.reshape(CHUNKS, slot_dev, slot_rows, chunk),
        w_in.reshape(slot_dev, 2, FF, width),
        w_out,
    )
    combined = pl.pallas_call(
        partial(return_kernel, depth, n_inner, planes),
        out_shape=jax.ShapeDtypeStruct((batches * tok_count, width), jnp.bfloat16),
        in_specs=[hbm, vmem, vmem],
        out_specs=vmem,
        scratch_shapes=[
            pltpu.VMEM((CHUNKS, planes, slot_dev, box_rows, chunk), jnp.bfloat16),
            pltpu.VMEM((count, rows), jnp.bfloat16),
            pltpu.VMEM((count, rows), jnp.bfloat16),
            pltpu.VMEM((depth, batches * tok_count, chunk), jnp.float32),
            pltpu.VMEM((CHUNKS, depth, batches * tok_count, chunk), jnp.bfloat16),
            pltpu.VMEM((CHUNKS, batches * tok_count, chunk), jnp.float32),
            pltpu.VMEM((CHUNKS, depth, batches * tok_count, chunk), jnp.bfloat16),
            sem((CHUNKS, planes)),
            sem((CHUNKS, planes)),
            sem((CHUNKS,)),
            sem((CHUNKS, depth)),
            sem((CHUNKS, depth)),
        ],
        compiler_params=pltpu.CompilerParams(
            collective_id=2, has_side_effects=True, vmem_limit_bytes=48 * 2**20
        ),
        name="give_back",
    )(served.reshape(CHUNKS, slot_dev, planes, box_rows, chunk), row, weight)
    return combined.reshape(batches, tok_count, width)


def local(
    tokens,
    route_weight,
    routes,
    replica,
    old_place,
    new_src,
    w_in,
    w_out,
    queries,
    latent_cache,
    block_req,
    block_len,
):
    slot_index = jnp.arange(old_place.shape[0], dtype=jnp.int32)
    keys = jnp.stack([replica_keys(old_place), replica_keys(table_lookup(new_src, old_place))])
    weight_slot = jnp.stack([slot_index, new_src])
    route_key = (routes * 2 + replica).reshape(2, -1)
    slots = jnp.sum(
        jnp.where(route_key[:, :, None] == keys[:, None, :], weight_slot[:, None, :], 0), axis=2
    )
    moe_out = moe(tokens, route_weight, slots, w_in, w_out)
    attend = jax.vmap(partial(block_attention, latent=LAT))
    req_max, req_total, req_out = attend(queries, latent_cache, block_req, block_len)
    attention = join_attention(req_max, req_total, req_out, "inner")
    return (moe_out, attention)


def solution(mesh):
    in_specs = (
        P(None, ("group", "inner"), None),
        P(None, ("group", "inner"), None),
        P(None, ("group", "inner"), None),
        P(None, ("group", "inner"), None),
        P(),
        P(),
        P(("group", "inner"), None, None),
        P(("group", "inner"), None, None),
        P(None, "group", None, None),
        P(None, ("group", "inner"), None, None),
        P(None, ("group", "inner")),
        P(None, ("group", "inner")),
    )
    out_specs = (P(None, ("group", "inner"), None), P(None, "group", None, None))
    return jax.shard_map(local, mesh=mesh, in_specs=in_specs, out_specs=out_specs, check_vma=False)
```

```python
from functools import partial

import jax
import jax.numpy as jnp
from jax import lax
from jax.experimental import pallas as pl
from jax.experimental.pallas import tpu as pltpu
from jax.sharding import PartitionSpec as P

MESH = pl.DeviceIdType.MESH
FF = 1408
EXPERTS = 64
TOPK = 6
LAT = 512
MOST = 6
CHUNKS = 4


score_scale = 192.0 ** (-0.5)
floor_value = -1e30


def block_attention(queries, latent_cache, block_req, block_len, latent):
    requests, head_count, feat_width = queries.shape
    blocks, cache_rows, _ = latent_cache.shape
    belongs = block_req[:, None] == jnp.arange(requests, dtype=jnp.int32)[None, :]
    chosen = jnp.dot(
        belongs.astype(jnp.bfloat16),
        queries.reshape(requests, head_count * feat_width),
        preferred_element_type=jnp.float32,
    )
    chosen = chosen.astype(jnp.bfloat16).reshape(blocks, head_count, feat_width)
    scores = (
        jnp.einsum("chk,cpk->chp", chosen, latent_cache, preferred_element_type=jnp.float32)
        * score_scale
    )
    live_rows = jnp.arange(cache_rows, dtype=jnp.int32)[None, :] < block_len[:, None]
    scores = jnp.where(live_rows[:, None, :], scores, floor_value)
    block_max = jnp.max(scores, axis=2)
    req_max = jnp.max(jnp.where(belongs[:, :, None], block_max[:, None, :], floor_value), axis=0)
    own_max = jnp.sum(jnp.where(belongs[:, :, None], req_max[None, :, :], 0.0), axis=1)
    exp_scores = jnp.where(live_rows[:, None, :], jnp.exp(scores - own_max[:, :, None]), 0.0)
    block_total = jnp.sum(exp_scores, axis=2)
    weights = exp_scores.astype(jnp.bfloat16)
    block_out = jnp.einsum(
        "chp,cpl->chl", weights, latent_cache[:, :, :latent], preferred_element_type=jnp.float32
    )
    belongs_f = belongs.astype(jnp.float32)
    req_total = jnp.einsum("cr,ch->rh", belongs_f, block_total, precision=lax.Precision.HIGHEST)
    req_out = jnp.einsum("cr,chl->rhl", belongs_f, block_out, precision=lax.Precision.HIGHEST)
    return (req_max, req_total, req_out)


def split_attention(req_max, req_total, req_out, n):
    batches, requests, heads, latent = req_out.shape
    share = batches * requests * heads // n
    stats = jnp.stack([req_max.reshape(n, share), req_total.reshape(n, share)], axis=2)
    stats = jnp.pad(stats, ((0, 0), (0, 0), (0, 126)))
    return stats, req_out.astype(jnp.bfloat16).reshape(n, share, latent)


def replica_keys(expert_of_slot):
    slots = expert_of_slot.shape[0]
    index = jnp.arange(slots, dtype=jnp.int32)
    earlier = (expert_of_slot[None, :] == expert_of_slot[:, None]) & (index[None, :] < index[:, None])
    return expert_of_slot * 2 + jnp.sum(earlier.astype(jnp.int32), axis=1)


def table_lookup(indices, lookup_table):
    matches = indices[:, None] == jnp.arange(lookup_table.shape[0], dtype=jnp.int32)[None, :]
    return jnp.sum(jnp.where(matches, lookup_table[None, :], 0), axis=1)


def places(depth, n_inner):
    width = n_inner // depth
    g, i = lax.axis_index("group"), lax.axis_index("inner")
    z, y = i // width, lax.rem(i, width)
    line = lambda p: (g, p * width + y)
    plane = lambda p: (p // width, z * width + lax.rem(p, width))
    return z, g * width + y, line, plane


def greet(partners):
    barrier = pltpu.get_barrier_semaphore()
    for device in partners:
        pl.semaphore_signal(barrier, inc=1, device_id=device, device_id_type=MESH)
    pl.semaphore_wait(barrier, len(partners))


def remote(src, dst, send, recv, device):
    return pltpu.make_async_remote_copy(
        src_ref=src, dst_ref=dst, send_sem=send, recv_sem=recv, device_id=device, device_id_type=MESH
    )


def dispatch_kernel(
    depth, n_inner, planes, tok, rid, rw, stats, parts, out, row_out, rw_out, whole,
    gat, tab, box, rowg, rwg, got_stats, got_parts, joined,
    zs, zr, ps, pr, ls, ms, mr, ws, wr, ss, sr, qs, qr, js, jr, jl,
):
    z, me, line, plane = places(depth, n_inner)
    line_to = [lax.rem(z + k, depth) for k in range(1, depth)]
    plane_to = [lax.rem(me + k, planes) for k in range(1, planes)]
    g, i = lax.axis_index("group"), lax.axis_index("inner")
    inner_to = [lax.rem(i + k, n_inner) for k in range(1, n_inner)]
    greet(
        [line(p) for p in line_to] + [plane(p) for p in plane_to] + [(g, p) for p in inner_to]
    )
    chunk = gat.shape[3]
    per_box = tab.shape[0] // planes
    metas, shares = [], []
    for k, p in enumerate(line_to):
        metas.append(remote(rid, rowg.at[z], ms.at[k], mr.at[k], line(p)))
        metas.append(remote(rw, rwg.at[z], ws.at[k], wr.at[k], line(p)))
    for copy in metas:
        copy.start()
    flights = []
    for c in range(CHUNKS):
        flight = []
        for k, p in enumerate(line_to):
            copy = remote(
                tok.at[:, pl.ds(c * chunk, chunk)], gat.at[c, z], zs.at[c, k], zr.at[c, k], line(p)
            )
            copy.start()
            flight.append(copy)
        flights.append(flight)
    for k, p in enumerate(inner_to):
        shares.append(remote(stats.at[p], got_stats.at[i], ss.at[k], sr.at[k], (g, p)))
        shares.append(remote(parts.at[p], got_parts.at[i], qs.at[k], qr.at[k], (g, p)))
    for copy in shares:
        copy.start()
    for c in range(CHUNKS):
        gat[c, z] = tok[:, c * chunk : (c + 1) * chunk]
    rowg[z] = rid[...]
    rwg[z] = rw[...]
    got_stats[i] = stats[i]
    got_parts[i] = parts[i]
    for copy in metas:
        copy.wait()
    row_out[...] = rowg[...]
    rw_out[...] = rwg[...]
    step = 256
    per_source = tok.shape[0]

    def fill(t, carry):
        first = t * step + z * tab.shape[0]
        rows = lax.broadcasted_iota(jnp.int32, (step, per_source), 0) + first
        for s in range(depth):
            total = jnp.zeros((step, per_source), jnp.float32)
            for k in range(TOPK):
                total = total + jnp.where(rows == rowg[s, k : k + 1, :], 1.0, 0.0)
            tab[
                pl.ds(pl.multiple_of(t * step, step), step), s * per_source : (s + 1) * per_source
            ] = total.astype(jnp.bfloat16)
        return carry

    lax.fori_loop(0, tab.shape[0] // step, fill, 0)
    sends = []
    for c in range(CHUNKS):
        for copy in flights[c]:
            copy.wait_recv()
        held = gat[c].reshape(tab.shape[1], chunk)

        def build(p, carry):
            table = tab[pl.ds(pl.multiple_of(p * per_box, 16), per_box), :]
            made = jnp.dot(table, held, preferred_element_type=jnp.float32).astype(jnp.bfloat16)
            box[c, p] = made.reshape(box.shape[2:])
            return carry

        lax.fori_loop(0, planes, build, 0)
        for k, p in enumerate(plane_to):
            copy = remote(box.at[c, p], out.at[c, :, me], ps.at[c, k], pr.at[c, k], plane(p))
            copy.start()
            sends.append(copy)
        own = pltpu.make_async_copy(box.at[c, me], out.at[c, :, me], ls.at[c])
        own.start()
        sends.append(own)
        if c == 0:
            for copy in shares:
                copy.wait()
            joint = got_stats[0, :, 0:1]
            for p in range(1, n_inner):
                joint = jnp.maximum(joint, got_stats[p, :, 0:1])
            total = jnp.zeros_like(joint)
            summed = jnp.zeros(joined.shape, jnp.float32)
            for p in range(n_inner):
                scale = jnp.exp(got_stats[p, :, 0:1] - joint)
                total = total + got_stats[p, :, 1:2] * scale
                summed = summed + got_parts[p].astype(jnp.float32) * scale
            joined[...] = (summed / total).astype(jnp.bfloat16)
            for k, p in enumerate(inner_to):
                copy = remote(joined, whole.at[i], js.at[k], jr.at[k], (g, p))
                copy.start()
                sends.append(copy)
            kept = pltpu.make_async_copy(joined, whole.at[i], jl)
            kept.start()
            sends.append(kept)
    for flight in flights:
        for copy in flight:
            copy.wait_send()
    for copy in sends:
        copy.wait()


def return_kernel(
    depth, n_inner, planes, served, row, weight, out, got, high, low, part, pbuf, own, back, ps, pr, ls, zs, zr
):
    z, me, line, plane = places(depth, n_inner)
    line_to = [lax.rem(z + k, depth) for k in range(1, depth)]
    plane_to = [lax.rem(me + k, planes) for k in range(1, planes)]
    greet([line(p) for p in line_to] + [plane(p) for p in plane_to])
    chunk = got.shape[-1]
    flights = []
    for c in range(CHUNKS):
        flight = []
        for k, p in enumerate(plane_to):
            copy = remote(served.at[c, :, p], got.at[c, me], ps.at[c, k], pr.at[c, k], plane(p))
            copy.start()
            flight.append(copy)
        kept = pltpu.make_async_copy(served.at[c, :, me], got.at[c, me], ls.at[c])
        kept.start()
        flight.append(kept)
        flights.append(flight)
    tokens, rows = high.shape
    step = 256
    for t in range(rows // step):
        cols = lax.broadcasted_iota(jnp.int32, (tokens, step), 1) + t * step
        total = jnp.zeros((tokens, step), jnp.float32)
        for k in range(TOPK):
            total = total + jnp.where(cols == row[:, k : k + 1], weight[:, k : k + 1], 0.0)
        upper = total.astype(jnp.bfloat16)
        high[:, t * step : (t + 1) * step] = upper
        low[:, t * step : (t + 1) * step] = (total - upper.astype(jnp.float32)).astype(jnp.bfloat16)
    sends = []
    for c in range(CHUNKS):
        for copy in flights[c]:
            copy.wait()
        held = got[c].reshape(rows, chunk)
        made = jnp.dot(high[...], held, preferred_element_type=jnp.float32)
        made = made + jnp.dot(low[...], held, preferred_element_type=jnp.float32)
        part[...] = made.reshape(part.shape)
        pbuf[c] = part[...].astype(jnp.bfloat16)
        own[c] = part[z]
        flight = []
        for k, p in enumerate(line_to):
            copy = remote(pbuf.at[c, p], back.at[c, z], zs.at[c, k], zr.at[c, k], line(p))
            copy.start()
            flight.append(copy)
        sends.append(flight)
    for c in range(CHUNKS):
        for copy in sends[c]:
            copy.wait()
        total = own[c]
        for p in line_to:
            total = total + back[c, p].astype(jnp.float32)
        out[:, c * chunk : (c + 1) * chunk] = total.astype(jnp.bfloat16)


def expert_kernel(tile, halves, x, w_gate_up, w_out, out, acc):
    half = pl.program_id(1)
    rows = x.shape[2]
    chunk = x.shape[3]
    for t in range(rows // tile):
        at = slice(t * tile, (t + 1) * tile)
        arrived = jnp.concatenate([x[c, 0, at, :] for c in range(CHUNKS)], axis=1)
        contract = (((1,), (1,)), ((), ()))
        gate = lax.dot_general(arrived, w_gate_up[0, 0], contract, preferred_element_type=jnp.float32)
        up = lax.dot_general(arrived, w_gate_up[0, 1], contract, preferred_element_type=jnp.float32)
        hidden = (gate / (1.0 + jnp.exp(-gate)) * up).astype(jnp.bfloat16)
        made = jnp.dot(hidden, w_out[0], preferred_element_type=jnp.float32)

        @pl.when(half == 0)
        def _():
            acc[at, :] = made

        @pl.when(half == halves - 1)
        def _():
            total = acc[at, :] + made
            for c in range(CHUNKS):
                out[c, 0, at, :] = total[:, c * chunk : (c + 1) * chunk].astype(jnp.bfloat16)


def layer(tokens, route_weight, slots, w_in, w_out, stats, parts):
    n_group, n_inner = lax.axis_size("group"), lax.axis_size("inner")
    batches, tok_count, width = tokens.shape
    slot_dev = w_in.shape[0]
    depth = 4 if n_inner % 4 == 0 else 1
    n_width = n_inner // depth
    planes = n_group * n_width
    box_rows = batches * depth * MOST
    rows = planes * slot_dev * box_rows
    count = depth * batches * tok_count
    chunk = width // CHUNKS
    order = jnp.arange(tok_count * TOPK, dtype=jnp.int32)
    same = (slots[:, :, None] == slots[:, None, :]) & (order[None, None, :] < order[None, :, None])
    position = jnp.sum(same.astype(jnp.int32), axis=2)
    device, local_slot = slots // slot_dev, slots % slot_dev
    dev_group, dev_inner = device // n_inner, device % n_inner
    plane = dev_group * n_width + dev_inner % n_width
    source = lax.axis_index("inner") // n_width
    batch = jnp.arange(batches, dtype=jnp.int32)[:, None]
    row = (plane * slot_dev + local_slot) * box_rows + (source * batches + batch) * MOST + position
    row = row + (dev_inner // n_width) * rows
    row = row.reshape(batches * tok_count, TOPK).T
    row = jnp.pad(row, ((0, 2), (0, 0)), constant_values=-1)
    weight = jnp.pad(route_weight.reshape(batches * tok_count, TOPK).T, ((0, 2), (0, 0)))
    vmem, hbm = pl.BlockSpec(memory_space=pltpu.VMEM), pl.BlockSpec(memory_space=pl.ANY)
    sem = pltpu.SemaphoreType.DMA
    per_source = batches * tok_count
    arrived, row, weight, attention = pl.pallas_call(
        partial(dispatch_kernel, depth, n_inner, planes),
        out_shape=(
            jax.ShapeDtypeStruct((CHUNKS, slot_dev, planes, box_rows, chunk), jnp.bfloat16),
            jax.ShapeDtypeStruct((depth, 8, per_source), jnp.int32),
            jax.ShapeDtypeStruct((depth, 8, per_source), jnp.float32),
            jax.ShapeDtypeStruct(parts.shape, jnp.bfloat16),
        ),
        in_specs=[vmem] * 5,
        out_specs=(hbm, vmem, vmem, hbm),
        scratch_shapes=[
            pltpu.VMEM((CHUNKS, depth, batches * tok_count, chunk), jnp.bfloat16),
            pltpu.VMEM((rows, count), jnp.bfloat16),
            pltpu.VMEM((CHUNKS, planes, slot_dev, box_rows, chunk), jnp.bfloat16),
            pltpu.VMEM((depth, 8, per_source), jnp.int32),
            pltpu.VMEM((depth, 8, per_source), jnp.float32),
            pltpu.VMEM(stats.shape, jnp.float32),
            pltpu.VMEM(parts.shape, jnp.bfloat16),
            pltpu.VMEM(parts.shape[1:], jnp.bfloat16),
            sem((CHUNKS, depth)),
            sem((CHUNKS, depth)),
            sem((CHUNKS, planes)),
            sem((CHUNKS, planes)),
            sem((CHUNKS,)),
        ]
        + [sem((depth,))] * 4
        + [sem((n_inner,))] * 6
        + [sem],
        compiler_params=pltpu.CompilerParams(
            collective_id=1, has_side_effects=True, vmem_limit_bytes=40 * 2**20
        ),
        name="dispatch",
    )(tokens.reshape(batches * tok_count, width), row, weight, stats, parts)
    first = (lax.axis_index("inner") // n_width) * rows
    row = row.transpose(0, 2, 1).reshape(count, 8) - first
    weight = weight.transpose(0, 2, 1).reshape(count, 8)
    halves = 2
    slot_rows = planes * box_rows
    tile = 384 if slot_rows % 384 == 0 else slot_rows
    mode = {} if slot_rows <= 384 else {"pipeline_mode": pl.Buffered(1)}
    part_ff = FF // halves
    act = pl.BlockSpec((CHUNKS, 1, slot_rows, chunk), lambda s, h: (0, s, 0, 0), **mode)
    served = pl.pallas_call(
        partial(expert_kernel, tile, halves),
        grid=(slot_dev, halves),
        out_shape=jax.ShapeDtypeStruct((CHUNKS, slot_dev, slot_rows, chunk), jnp.bfloat16),
        in_specs=[
            act,
            pl.BlockSpec((1, 2, part_ff, width), lambda s, h: (s, 0, h, 0)),
            pl.BlockSpec((1, part_ff, width), lambda s, h: (s, h, 0)),
        ],
        out_specs=act,
        scratch_shapes=[pltpu.VMEM((slot_rows, width), jnp.float32)],
        compiler_params=pltpu.CompilerParams(
            vmem_limit_bytes=60 * 2**20, dimension_semantics=("arbitrary", "arbitrary")
        ),
        cost_estimate=pl.CostEstimate(
            flops=6 * slot_dev * slot_rows * FF * width,
            bytes_accessed=6 * slot_dev * FF * width,
            transcendentals=0,
        ),
        name="experts",
    )(
        arrived.reshape(CHUNKS, slot_dev, slot_rows, chunk),
        w_in.reshape(slot_dev, 2, FF, width),
        w_out,
    )
    combined = pl.pallas_call(
        partial(return_kernel, depth, n_inner, planes),
        out_shape=jax.ShapeDtypeStruct((batches * tok_count, width), jnp.bfloat16),
        in_specs=[hbm, vmem, vmem],
        out_specs=vmem,
        scratch_shapes=[
            pltpu.VMEM((CHUNKS, planes, slot_dev, box_rows, chunk), jnp.bfloat16),
            pltpu.VMEM((count, rows), jnp.bfloat16),
            pltpu.VMEM((count, rows), jnp.bfloat16),
            pltpu.VMEM((depth, batches * tok_count, chunk), jnp.float32),
            pltpu.VMEM((CHUNKS, depth, batches * tok_count, chunk), jnp.bfloat16),
            pltpu.VMEM((CHUNKS, batches * tok_count, chunk), jnp.float32),
            pltpu.VMEM((CHUNKS, depth, batches * tok_count, chunk), jnp.bfloat16),
            sem((CHUNKS, planes)),
            sem((CHUNKS, planes)),
            sem((CHUNKS,)),
            sem((CHUNKS, depth)),
            sem((CHUNKS, depth)),
        ],
        compiler_params=pltpu.CompilerParams(
            collective_id=2, has_side_effects=True, vmem_limit_bytes=48 * 2**20
        ),
        name="give_back",
    )(served.reshape(CHUNKS, slot_dev, planes, box_rows, chunk), row, weight)
    return combined.reshape(batches, tok_count, width), attention


def local(
    tokens,
    route_weight,
    routes,
    replica,
    old_place,
    new_src,
    w_in,
    w_out,
    queries,
    latent_cache,
    block_req,
    block_len,
):
    slot_index = jnp.arange(old_place.shape[0], dtype=jnp.int32)
    keys = jnp.stack([replica_keys(old_place), replica_keys(table_lookup(new_src, old_place))])
    weight_slot = jnp.stack([slot_index, new_src])
    route_key = (routes * 2 + replica).reshape(2, -1)
    slots = jnp.sum(
        jnp.where(route_key[:, :, None] == keys[:, None, :], weight_slot[:, None, :], 0), axis=2
    )
    attend = jax.vmap(partial(block_attention, latent=LAT))
    partial_attention = attend(queries, latent_cache, block_req, block_len)
    stats, parts = split_attention(*partial_attention, lax.axis_size("inner"))
    moe_out, attention = layer(tokens, route_weight, slots, w_in, w_out, stats, parts)
    attention = attention.reshape(queries.shape[:3] + (LAT,))
    return (moe_out, attention)


def solution(mesh):
    in_specs = (
        P(None, ("group", "inner"), None),
        P(None, ("group", "inner"), None),
        P(None, ("group", "inner"), None),
        P(None, ("group", "inner"), None),
        P(),
        P(),
        P(("group", "inner"), None, None),
        P(("group", "inner"), None, None),
        P(None, "group", None, None),
        P(None, ("group", "inner"), None, None),
        P(None, ("group", "inner")),
        P(None, ("group", "inner")),
    )
    out_specs = (P(None, ("group", "inner"), None), P(None, "group", None, None))
    return jax.shard_map(local, mesh=mesh, in_specs=in_specs, out_specs=out_specs, check_vma=False)
```
